32 devices in a mesh: row: 8 (over y, x, core), col: 4 (over z).
Axes of the slice: x: 2, y: 2, z: 4, core: 2. Of those that a mesh axis runs over, the one named last changes fastest.
Arguments:
- struct_basis: float32 [8192, 1024], P(('row', 'col')), may hold values from -6 to 6
- fluid_basis: float32 [4096, 1024], P(('row', 'col')), may hold values from -6 to 6
- stiff_tiles: float32 [64, 4, 128, 128], P(('row', 'col')), may hold values from -0.0029296875 to 0.0029296875
- mass_tiles: float32 [64, 4, 128, 128], P(('row', 'col')), may hold values from -0.0029296875 to 0.0029296875
- fluid_stiff_tiles: float32 [32, 4, 128, 128], P(('row', 'col')), may hold values from -0.00390625 to 0.00390625
- fluid_mass_tiles: float32 [32, 4, 128, 128], P(('row', 'col')), may hold values from -0.00390625 to 0.00390625
- struct_cols: int32 [64, 4], P(('row', 'col')), may hold values from 0 to 3
- fluid_cols: int32 [32, 4], P(('row', 'col')), may hold values from 0 to 2
- wet_rows: int32 [1024], P(('row', 'col')), may hold values from 0 to 127
- wet_dest: int32 [1024, 1], P(('row', 'col')), may hold values from 0 to 31; in each aligned block of 32 rows (0 to 31, 32 to 63, ...) at most 2 rows name the same one
- coupling: float32 [8192, 64], P(('row', 'col')), may hold values from -0.0078125 to 0.0078125
Outputs:
- stiff_red: float32 [1024, 1024], P('row', 'col')
- mass_red: float32 [1024, 1024], P('row', 'col')
- fluid_stiff_red: float32 [1024, 1024], P('row', 'col')
- fluid_mass_red: float32 [1024, 1024], P('row', 'col')
- coupling_red: float32 [1024, 1024], P('row', 'col')
The draws below stay inside these ranges and needn't reach their ends.
Inputs may be any that keep to these rules, and one draw needn't show every extreme that they name: `wet_dest`: among the 32 entries of one block, no block number is named more than 2 times, and some block number is named exactly 2 times in every draw.
All inputs are finite; a program needn't handle non-finite values.
Results may differ from the reference program's by a relative error of at most 0.0003.
Values sent between devices are 32-bit elements; how exact they have to be, the bound alone decides.
A program may use at most 128 MiB of HBM per device.

```python
import math
import jax
import jax.numpy as jnp
import numpy as np
from jax import lax

R = 1024
TILE = 128
NB = 4
HALO = 1
CAP = 2
STILE_DEV = 2
ATILE_DEV = 1
SHARDS = 32
WET_DEV = 32
AROWS_DEV = 128
NS = 8192
NA = 4096
NREC = 64
N_ROW = 8
N_COL = 4


def with_ends(values, key, low, largest):
    place = [jax.random.randint(jax.random.fold_in(key, axis), (), 0, length) for axis, length in enumerate(values.shape)]
    widest = values.shape.index(max(values.shape))
    neighbour = place[:widest] + [(place[widest] + 1) % values.shape[widest]] + place[widest + 1:]
    return values.at[tuple(place)].set(low).at[tuple(neighbour)].set(largest)


def with_spikes(entries, stream_key, source, target, blocks, factor):
    owner, partner = [(jnp.arange(entries.shape[axis_at]) // (entries.shape[axis_at] // blocks)).reshape([-1 if axis == axis_at else 1 for axis in range(entries.ndim)]) for axis_at in (source, target)]
    chosen = jax.random.permutation(stream_key, blocks)[partner]
    strong = (owner == chosen) | (owner == (partner + blocks // 2) % blocks)
    return jnp.where(strong, factor * entries, entries)


def block_levels(own_key, shape, cuts, least, high):
    level, own = 1.0, jax.random.fold_in(own_key, 6)
    for position, blocks in cuts:
        draws = jnp.exp(jax.random.uniform(jax.random.fold_in(own, position), (blocks,), jnp.float32, least / len(cuts), high / len(cuts)))
        level = level * jnp.repeat(draws, shape[position] // blocks).reshape([-1 if axis == position else 1 for axis in range(len(shape))])
    return level


def assign_block(stream_key, own, number, rows, count, top, bound, lean):
    order = jax.random.permutation(stream_key, count)
    packed, common = load_shares(count, rows * top, bound, lean, True), load_shares(count, rows * top, bound, lean, False)
    places = jnp.arange(count)

    def named(lengths, rotation):
        used = int((lengths > 0).sum())
        fixed = max(1, used // 4)
        moved = fixed + (places - fixed + rotation * (used - fixed)) % max(1, count - fixed)
        return jnp.zeros((count,), jnp.int32).at[order[jnp.where(places < fixed, places, moved)]].set(jnp.asarray(lengths, jnp.int32))

    lengths = jnp.where(number % 4 == 0, named(packed, number // 4), named(common, number - number // 4 - 1))
    mixed = jax.random.permutation(jax.random.fold_in(own, 3), count)
    donor, receiver = mixed[0:count // 2 * 2:2], mixed[1:count // 2 * 2:2]
    margin = jnp.minimum(lengths[donor] - 1, bound - lengths[receiver]) // 2
    margin = jnp.where((donor == order[0]) | (receiver == order[0]) | (lengths[receiver] == 0), 0, jnp.maximum(margin, 0))
    moved = jax.random.randint(jax.random.fold_in(own, 4), (count // 2,), 0, 1 << 20) % (margin + 1)
    lengths = lengths.at[donor].add(-moved).at[receiver].add(moved)
    labels = jnp.searchsorted(jnp.cumsum(lengths), jnp.arange(rows * top), side="right").astype(jnp.int32)
    table = labels.reshape(top, rows).T
    table = table[jax.random.permutation(jax.random.fold_in(own, 1), rows)]
    rotation = jax.random.randint(jax.random.fold_in(own, 2), (rows, 1), 0, top)
    return jnp.take_along_axis(table, (jnp.arange(top)[None, :] + rotation) % top, axis=1)


def load_shares(amount, total, limit, skew, full):
    loads = [(1 << 20) // math.isqrt(standing ** skew) + 1 for standing in range(1, amount + 1)]
    largest = limit if full else min(limit, max(-(-total // amount), total * loads[0] // sum(loads)))
    least = 1 if total - largest >= amount - 1 else 0
    given, rest = [largest] + [least] * (amount - 1), total - largest - least * (amount - 1)
    while rest > 0:
        candidates = [i for i in range(1, amount) if given[i] < largest] or [i for i in range(1, amount) if given[i] < limit]
        pool, budget = sum([loads[i] for i in candidates]), rest
        for i in candidates:
            extra = min(limit - given[i], max(1, budget * loads[i] // pool), rest)
            given[i] = given[i] + extra
            rest = rest - extra
    return np.array(given)


def noise(key, shape, deviation, most, shards=(), kind=jnp.bfloat16):
    values = jax.random.normal(key, shape, jnp.float32) * deviation
    if len(shards) > 0:
        values = block_levels(key, shape, shards, -0.22, 0.18) * values
    return jnp.clip(values, min=-most, max=most).astype(kind)


def noise_with(own_key, shape, scale, reach, shards, heavy, held_as=jnp.bfloat16):
    values = scale * jax.random.normal(own_key, shape, jnp.float32)
    if shards:
        values = values * block_levels(own_key, shape, shards, -0.22, 0.18)
    return jnp.clip(with_spikes(values, jax.random.fold_in(own_key, 3), *heavy), -reach, reach).astype(held_as)


def setup_inputs(seed: int = 0) -> dict:
    streams_of = jax.random.split(jax.random.key(seed), 12)
    struct_basis = noise_with(streams_of[0], (NS, R), 1.0, 6.0, ((0, 32),), (0, 1, 32, 2.75), jnp.float32)
    fluid_basis = noise_with(streams_of[1], (NA, R), 1.0, 6.0, ((0, 32),), (0, 1, 32, 2.75), jnp.float32)
    stiff_tiles = noise(streams_of[2], (STILE_DEV * SHARDS, NB, TILE, TILE), (TILE * NB * NS) ** -0.5, 0.0029296875, ((0, 32),), jnp.float32)
    mass_tiles = noise(streams_of[3], (STILE_DEV * SHARDS, NB, TILE, TILE), (TILE * NB * NS) ** -0.5, 0.0029296875, ((0, 32),), jnp.float32)
    fluid_stiff_tiles = noise(streams_of[4], (ATILE_DEV * SHARDS, NB, TILE, TILE), (TILE * NB * NA) ** -0.5, 0.00390625, ((0, 32),), jnp.float32)
    fluid_mass_tiles = noise(streams_of[5], (ATILE_DEV * SHARDS, NB, TILE, TILE), (TILE * NB * NA) ** -0.5, 0.00390625, ((0, 32),), jnp.float32)
    struct_cols = with_ends(jax.random.randint(streams_of[6], (STILE_DEV * SHARDS, NB), 0, STILE_DEV + 2 * HALO), jax.random.fold_in(streams_of[6], 1), 0, (STILE_DEV + 2 * HALO) - 1).astype(jnp.int32)
    fluid_cols = with_ends(jax.random.randint(streams_of[7], (ATILE_DEV * SHARDS, NB), 0, ATILE_DEV + 2 * HALO), jax.random.fold_in(streams_of[7], 1), 0, (ATILE_DEV + 2 * HALO) - 1).astype(jnp.int32)
    wet_rows = with_ends(jax.random.randint(streams_of[8], (WET_DEV * SHARDS,), 0, AROWS_DEV), jax.random.fold_in(streams_of[8], 1), 0, AROWS_DEV - 1).astype(jnp.int32)
    wet_dest_keys = jax.random.split(jax.random.fold_in(streams_of[9], 1), (WET_DEV * SHARDS) // WET_DEV)
    wet_dest_turns = jax.random.permutation(jax.random.fold_in(streams_of[9], 3), (WET_DEV * SHARDS) // WET_DEV)
    wet_dest = jax.vmap(lambda own, number: assign_block(jax.random.fold_in(streams_of[9], 2), own, number, WET_DEV, SHARDS, 1, CAP, 2))(wet_dest_keys, wet_dest_turns).reshape((WET_DEV * SHARDS, 1))
    coupling = noise(streams_of[10], (NS, NREC), (NS * SHARDS * CAP) ** -0.5, 0.0078125, ((0, 32),), jnp.float32)
    return dict(struct_basis=struct_basis, fluid_basis=fluid_basis, stiff_tiles=stiff_tiles, mass_tiles=mass_tiles, fluid_stiff_tiles=fluid_stiff_tiles, fluid_mass_tiles=fluid_mass_tiles, struct_cols=struct_cols, fluid_cols=fluid_cols, wet_rows=wet_rows, wet_dest=wet_dest, coupling=coupling)


exact_precision = lax.Precision.HIGHEST


def tile_product(tiles, columns, extended):
    blocks = extended.reshape(-1, TILE, R)
    picked = jnp.take(blocks, columns, axis=0)
    result = jnp.einsum("tbij,tbjr->tir", tiles, picked, precision=exact_precision)
    return result.reshape(-1, R)


def congruence(left_basis, image):
    return jnp.einsum("nr,ns->rs", left_basis, image, precision=exact_precision)


def slot_numbers(targets):
    shard_count = N_ROW * N_COL
    onehot = (targets[:, None] == jnp.arange(shard_count, dtype=jnp.int32)[None, :]).astype(jnp.int32)
    before = jnp.cumsum(onehot, axis=0) - onehot
    return jnp.sum(before * onehot, axis=1).astype(jnp.int32)


def extend(basis, device, height):
    shard_count = N_ROW * N_COL
    border = HALO * TILE
    total_rows = basis.shape[0]
    start = (device * height).astype(jnp.int32)
    own_block = lax.dynamic_slice_in_dim(basis, start, height, 0)
    lower = lax.dynamic_slice_in_dim(basis, jnp.maximum(start - border, 0).astype(jnp.int32), border, 0)
    upper = lax.dynamic_slice_in_dim(basis, jnp.minimum(start + height, total_rows - border).astype(jnp.int32), border, 0)
    lower = lower * (device > 0).astype(basis.dtype)
    upper = upper * (device < shard_count - 1).astype(basis.dtype)
    return own_block, jnp.concatenate([lower, own_block, upper], axis=0)


def reference(struct_basis, fluid_basis, stiff_tiles, mass_tiles, fluid_stiff_tiles, fluid_mass_tiles, struct_cols, fluid_cols, wet_rows, wet_dest, coupling):
    shard_count = N_ROW * N_COL
    struct_height = STILE_DEV * TILE
    fluid_height = ATILE_DEV * TILE
    slot_total = shard_count * CAP
    destination = wet_dest[:, 0].reshape(shard_count, WET_DEV)
    slot_index = lax.map(slot_numbers, destination)
    source = jnp.arange(shard_count, dtype=jnp.int32)[:, None]
    target = (source * CAP + slot_index).reshape(-1).astype(jnp.int32)
    flat_dest = destination.reshape(-1)
    global_rows = (source * fluid_height + wet_rows.reshape(shard_count, WET_DEV)).reshape(-1).astype(jnp.int32)
    wet_values = jnp.take(fluid_basis, global_rows, axis=0)

    def step(totals, device):
        def device_part(array, count):
            return lax.dynamic_slice_in_dim(array, (device * count).astype(jnp.int32), count, 0)

        own_struct, extended_struct = extend(struct_basis, device, struct_height)
        own_fluid, extended_fluid = extend(fluid_basis, device, fluid_height)
        stiff_part = congruence(own_struct, tile_product(device_part(stiff_tiles, STILE_DEV), device_part(struct_cols, STILE_DEV), extended_struct))
        mass_part = congruence(own_struct, tile_product(device_part(mass_tiles, STILE_DEV), device_part(struct_cols, STILE_DEV), extended_struct))
        fstiff_part = congruence(own_fluid, tile_product(device_part(fluid_stiff_tiles, ATILE_DEV), device_part(fluid_cols, ATILE_DEV), extended_fluid))
        fmass_part = congruence(own_fluid, tile_product(device_part(fluid_mass_tiles, ATILE_DEV), device_part(fluid_cols, ATILE_DEV), extended_fluid))
        places = jnp.where(flat_dest == device, target, slot_total).astype(jnp.int32)
        received = jnp.zeros((slot_total, R), fluid_basis.dtype).at[places].set(wet_values, mode="drop")
        projected = jnp.einsum("nr,nk->rk", own_struct, device_part(coupling, struct_height), precision=exact_precision)
        coupled_part = jnp.dot(projected, received, precision=exact_precision)
        updated = (totals[0] + stiff_part, totals[1] + mass_part, totals[2] + fstiff_part, totals[3] + fmass_part, totals[4] + coupled_part)
        return updated, None

    empty_sum = jnp.zeros((R, R), struct_basis.dtype)
    totals, unused = lax.scan(step, (empty_sum, empty_sum, empty_sum, empty_sum, empty_sum), jnp.arange(shard_count, dtype=jnp.int32))
    return (totals[0], totals[1], totals[2], totals[3], totals[4])
```

```python
import functools

import jax
import jax.numpy as jnp
from jax import lax
from jax.experimental import pallas as pl
from jax.experimental.pallas import tpu as pltpu
from jax.sharding import PartitionSpec as P

TILE = 128
HALO = 1
CAP = 2
MATS = 5
VMEM_LIMIT = 67043328
MESH = pl.DeviceIdType.MESH

exact_precision = lax.Precision.HIGHEST


def halves(value):
    high = value.astype(jnp.bfloat16)
    low = (value - high.astype(jnp.float32)).astype(jnp.bfloat16)
    return high, low


def bits_of(size):
    return size.bit_length() - 1


def subset_offsets(bits):
    offsets = [0]
    for bit in bits:
        offsets = [base + extra for extra in (0, 1 << bit) for base in offsets]
    return offsets


def kernel(
    nr,
    nc,
    struct_cols,
    fluid_cols,
    struct,
    fluid,
    stiff_tiles,
    mass_tiles,
    fstiff_tiles,
    fmass_tiles,
    coupling,
    received,
    *refs,
):
    outs = refs[:MATS]
    acc, halo_s, halo_f, left_s, left_f, tiles_s, tiles_f, ext_s, ext_f, image = refs[MATS : MATS + 10]
    landing = refs[MATS + 10 : -4]
    send_sem, recv_sem, halo_send, halo_recv = refs[-4:]
    rows_s, size = struct.shape
    rows_f = fluid.shape[0]
    bm, bn = size // nr, size // nc
    hb = bm // 2
    border = TILE * HALO
    shards = nr * nc
    row, col = lax.axis_index("row"), lax.axis_index("col")
    block = row * nc + col
    following = lax.rem(block + 1, shards)
    previous = lax.rem(block + shards - 1, shards)
    after = (following // nc, lax.rem(following, nc))
    before = (previous // nc, lax.rem(previous, nc))
    row_bits, col_bits = bits_of(nr), bits_of(nc)
    stages = row_bits + col_bits
    my_row = [lax.rem(row // (1 << b), 2) for b in range(row_bits)]
    my_col = [lax.rem(col // (1 << b), 2) for b in range(col_bits)]
    row_peer = [(row + (1 - 2 * my_row[b]) * (1 << b), col) for b in range(row_bits)]
    col_peer = [(row, col + (1 - 2 * my_col[b]) * (1 << b)) for b in range(col_bits)]

    barrier = pltpu.get_barrier_semaphore()
    greeted = [after, before] + row_peer + col_peer
    for device in greeted:
        pl.semaphore_signal(barrier, inc=1, device_id=device, device_id_type=MESH)
    pl.semaphore_wait(barrier, len(greeted))

    def halo_copy(number, source, target, device):
        return pltpu.make_async_remote_copy(
            src_ref=source,
            dst_ref=target,
            send_sem=halo_send.at[number],
            recv_sem=halo_recv.at[number],
            device_id=device,
            device_id_type=MESH,
        )

    halos = [
        halo_copy(0, struct.at[pl.ds(rows_s - border, border)], halo_s.at[0], after),
        halo_copy(1, struct.at[pl.ds(0, border)], halo_s.at[1], before),
        halo_copy(2, fluid.at[pl.ds(rows_f - border, border)], halo_f.at[0], after),
        halo_copy(3, fluid.at[pl.ds(0, border)], halo_f.at[1], before),
    ]
    for copy in halos:
        copy.start()

    def row_order(half):
        order = list(range(row_bits))
        return order if half == 0 else order[:1] + order[1:][::-1]

    def exchange(half, mat, stage):
        if stage < row_bits:
            order, mine, peers, at = row_order(half), my_row, row_peer, stage
        else:
            order, mine, peers, at = list(range(col_bits)), my_col, col_peer, stage - row_bits
        fixed = sum((mine[b] * (1 << b) for b in order[:at]), 0)
        bit = order[at]
        rest = subset_offsets(order[at + 1 :])
        sent = [fixed + (1 - mine[bit]) * (1 << bit) + extra for extra in rest]
        kept = [fixed + mine[bit] * (1 << bit) + extra for extra in rest]
        return sent, kept, peers[bit]

    def whole_stage(half, mat, stage):
        peer = exchange(half, mat, stage)[2]
        return pltpu.make_async_remote_copy(
            src_ref=landing[stage].at[half, mat],
            dst_ref=landing[stage].at[half, mat],
            send_sem=send_sem.at[half, mat, stage],
            recv_sem=recv_sem.at[half, mat, stage],
            device_id=peer,
            device_id_type=MESH,
        )

    def send(half, mat, stage):
        sent, kept, peer = exchange(half, mat, stage)
        for place, index in enumerate(sent):
            if stage < row_bits:
                source = acc.at[half, mat, index]
            else:
                source = acc.at[half, mat, row, index]
            pltpu.make_async_remote_copy(
                src_ref=source,
                dst_ref=landing[stage].at[half, mat, place],
                send_sem=send_sem.at[half, mat, stage],
                recv_sem=recv_sem.at[half, mat, stage],
                device_id=peer,
                device_id_type=MESH,
            ).start()

    def absorb(half, mat, stage):
        sent, kept, peer = exchange(half, mat, stage)
        whole_stage(half, mat, stage).wait_recv()
        for place, index in enumerate(kept):
            if stage < row_bits:

                def add(c, carry, place=place, index=index):
                    acc[half, mat, index, c] = acc[half, mat, index, c] + landing[stage][half, mat, place, c]
                    return carry

                lax.fori_loop(0, nc, add, 0)
            elif stage < stages - 1:
                acc[half, mat, row, index] = acc[half, mat, row, index] + landing[stage][half, mat, place]
            else:
                outs[mat][pl.ds(half * hb, hb), :] = acc[half, mat, row, index] + landing[stage][half, mat, place]
        if stage < stages - 1:
            send(half, mat, stage + 1)

    def transpose_into(left, source, count):
        def step(k, carry):
            at = pl.ds(pl.multiple_of(k * TILE, TILE), TILE)
            high, low = halves(source[:, at].T)
            left[at, pl.ds(0, count)] = high
            left[at, pl.ds(count, count)] = high
            left[at, pl.ds(2 * count, count)] = low
            return carry

        lax.fori_loop(0, size // TILE, step, 0)

    def columns(c):
        return pl.ds(pl.multiple_of(c * bn, bn), bn)

    def store_image(value, at, count):
        high, low = halves(value)
        image[pl.ds(0, count), at] = high
        image[pl.ds(count, count), at] = low
        image[pl.ds(2 * count, count), at] = high

    def project(left, count, mat):
        def step(c, carry):
            part = jnp.dot(
                left[...], image[pl.ds(0, 3 * count), columns(c)], preferred_element_type=jnp.float32
            )
            for r in range(nr):
                for half in range(2):
                    start = r * bm + half * hb
                    acc[half, mat, r, c] = part[start : start + hb]
            return carry

        lax.fori_loop(0, nc, step, 0)
        for half in range(2):
            send(half, mat, 0)

    def coupled():
        ch, cl = halves(coupling[...])

        def step(c, carry):
            at = columns(c)
            rh, rl = halves(received[:, at])
            value = jnp.dot(ch, rh, preferred_element_type=jnp.float32)
            value += jnp.dot(ch, rl, preferred_element_type=jnp.float32)
            value += jnp.dot(cl, rh, preferred_element_type=jnp.float32)
            store_image(value, at, rows_s)
            return carry

        lax.fori_loop(0, nc, step, 0)
        project(left_s, rows_s, 0)

    def place_rows(ext, total, start, value):
        count = value.shape[0]
        high, low = halves(value)
        ext[pl.ds(start, count), :] = high
        ext[pl.ds(total + start, count), :] = low
        ext[pl.ds(2 * total + start, count), :] = high

    def fill_ext(ext, own, halo, first, second):
        total = own.shape[0] + 2 * border
        place_rows(ext, total, border, own[...])
        halos[first].wait_recv()
        halos[second].wait_recv()
        place_rows(ext, total, 0, jnp.where(block > 0, halo[0], 0.0))
        place_rows(ext, total, total - border, jnp.where(block < shards - 1, halo[1], 0.0))

    def sparse_image(tiles, cols, dense, ext, rows, left, mat):
        total = rows + 2 * border
        for i in range(rows // TILE):
            for c in range(total // TILE):
                tile = jnp.zeros((TILE, TILE), jnp.float32)
                for k in range(tiles.shape[1]):
                    tile += jnp.where(cols[i, k] == c, tiles[i, k], 0.0)
                high, low = halves(tile)
                at = pl.ds(i * TILE, TILE)
                dense[at, pl.ds(c * TILE, TILE)] = high
                dense[at, pl.ds(total + c * TILE, TILE)] = high
                dense[at, pl.ds(2 * total + c * TILE, TILE)] = low

        def step(c, carry):
            at = columns(c)
            store_image(jnp.dot(dense[...], ext[:, at], preferred_element_type=jnp.float32), at, rows)
            return carry

        lax.fori_loop(0, nc, step, 0)
        project(left, rows, mat)

    def compute(mat):
        if mat == 0:
            transpose_into(left_s, struct, rows_s)
            coupled()
        elif mat == 1:
            fill_ext(ext_s, struct, halo_s, 0, 1)
            sparse_image(stiff_tiles, struct_cols, tiles_s, ext_s, rows_s, left_s, 1)
        elif mat == 2:
            sparse_image(mass_tiles, struct_cols, tiles_s, ext_s, rows_s, left_s, 2)
        elif mat == 3:
            transpose_into(left_f, fluid, rows_f)
            fill_ext(ext_f, fluid, halo_f, 2, 3)
            sparse_image(fstiff_tiles, fluid_cols, tiles_f, ext_f, rows_f, left_f, 3)
        else:
            sparse_image(fmass_tiles, fluid_cols, tiles_f, ext_f, rows_f, left_f, 4)

    for step in range(MATS + stages):
        if step < MATS:
            compute(step)
        for stage in range(stages):
            mat = step - 1 - stage
            if 0 <= mat < MATS:
                for half in range(2):
                    absorb(half, mat, stage)

    for copy in halos:
        copy.wait_send()
    for mat in range(MATS):
        for half in range(2):
            for stage in range(stages):
                whole_stage(half, mat, stage).wait_send()


def reduced(nr, nc, struct_cols, fluid_cols, *operands):
    struct, fluid = operands[0], operands[1]
    rows_s, size = struct.shape
    rows_f = fluid.shape[0]
    bm, bn = size // nr, size // nc
    hb = bm // 2
    row_bits, col_bits = bits_of(nr), bits_of(nc)
    stages = row_bits + col_bits
    border = TILE * HALO
    total_s, total_f = rows_s + 2 * border, rows_f + 2 * border
    f32, bf16 = jnp.float32, jnp.bfloat16
    landing = [pltpu.VMEM((2, MATS, nr >> (s + 1), nc, hb, bn), f32) for s in range(row_bits)]
    landing += [pltpu.VMEM((2, MATS, nc >> (s + 1), hb, bn), f32) for s in range(col_bits)]
    smem = pl.BlockSpec(memory_space=pltpu.SMEM)
    vmem = pl.BlockSpec(memory_space=pltpu.VMEM)
    return pl.pallas_call(
        functools.partial(kernel, nr, nc),
        out_shape=[jax.ShapeDtypeStruct((bm, bn), f32)] * MATS,
        in_specs=[smem, smem] + [vmem] * len(operands),
        out_specs=[vmem] * MATS,
        scratch_shapes=[
            pltpu.VMEM((2, MATS, nr, nc, hb, bn), f32),
            pltpu.VMEM((2, border, size), f32),
            pltpu.VMEM((2, border, size), f32),
            pltpu.VMEM((size, 3 * rows_s), bf16),
            pltpu.VMEM((size, 3 * rows_f), bf16),
            pltpu.VMEM((rows_s, 3 * total_s), bf16),
            pltpu.VMEM((rows_f, 3 * total_f), bf16),
            pltpu.VMEM((3 * total_s, size), bf16),
            pltpu.VMEM((3 * total_f, size), bf16),
            pltpu.VMEM((3 * rows_s, size), bf16),
            *landing,
            pltpu.SemaphoreType.DMA((2, MATS, stages)),
            pltpu.SemaphoreType.DMA((2, MATS, stages)),
            pltpu.SemaphoreType.DMA((4,)),
            pltpu.SemaphoreType.DMA((4,)),
        ],
        compiler_params=pltpu.CompilerParams(
            collective_id=0, has_side_effects=True, vmem_limit_bytes=VMEM_LIMIT
        ),
        name="reduced",
    )(struct_cols, fluid_cols, *operands)


def on_device(
    nr,
    nc,
    struct_basis,
    fluid_basis,
    stiff_tiles,
    mass_tiles,
    fluid_stiff_tiles,
    fluid_mass_tiles,
    struct_cols,
    fluid_cols,
    wet_rows,
    wet_dest,
    coupling,
):
    shards = nr * nc
    destination = wet_dest[:, 0]
    same = destination[:, None] == destination[None, :]
    entry = jnp.arange(destination.shape[0], dtype=jnp.int32)
    earlier = entry[None, :] < entry[:, None]
    slot_index = jnp.sum((same & earlier).astype(jnp.int32), axis=1)
    target = destination * CAP + slot_index
    fluid_row = jnp.arange(fluid_basis.shape[0], dtype=jnp.int32)
    slots = jnp.arange(shards * CAP, dtype=jnp.int32)
    hit = (slots[:, None, None] == target[None, None, :]) & (fluid_row[None, :, None] == wet_rows[None, None, :])
    selector = jnp.any(hit, axis=2).astype(jnp.float32)
    outgoing = jnp.dot(selector, fluid_basis, precision=exact_precision)
    received = lax.all_to_all(outgoing, ("row", "col"), split_axis=0, concat_axis=0, tiled=True)
    coupling_red, stiff_red, mass_red, fstiff_red, fmass_red = reduced(
        nr,
        nc,
        struct_cols,
        fluid_cols,
        struct_basis,
        fluid_basis,
        stiff_tiles,
        mass_tiles,
        fluid_stiff_tiles,
        fluid_mass_tiles,
        coupling,
        received,
    )
    return stiff_red, mass_red, fstiff_red, fmass_red, coupling_red


def solution(mesh):
    tiled = P(("row", "col"), None, None, None)
    lined = P(("row", "col"), None)
    return jax.shard_map(
        functools.partial(on_device, mesh.shape["row"], mesh.shape["col"]),
        mesh=mesh,
        in_specs=(lined, lined, tiled, tiled, tiled, tiled, lined, lined, P(("row", "col")), lined, lined),
        out_specs=(P("row", "col"),) * 5,
        check_vma=False,
    )
```

```python
import functools

import jax
import jax.numpy as jnp
from jax import lax
from jax.experimental import pallas as pl
from jax.experimental.pallas import tpu as pltpu
from jax.sharding import PartitionSpec as P

TILE = 128
HALO = 1
CAP = 2
MATS = 5
PARTS = 4
VMEM_LIMIT = 67043328
MESH = pl.DeviceIdType.MESH


def halves(value):
    high = value.astype(jnp.bfloat16)
    low = (value - high.astype(jnp.float32)).astype(jnp.bfloat16)
    return high, low


def bits_of(size):
    return size.bit_length() - 1


def subset_offsets(bits):
    offsets = [0]
    for bit in bits:
        offsets = [base + extra for extra in (0, 1 << bit) for base in offsets]
    return offsets


def kernel(
    nr,
    nc,
    struct_cols,
    fluid_cols,
    struct,
    fluid,
    stiff_tiles,
    mass_tiles,
    fstiff_tiles,
    fmass_tiles,
    coupling,
    selector,
    *refs,
):
    outs = refs[:MATS]
    acc, halo_s, halo_f, left_s, left_f, tiles_s, tiles_f, ext_s, ext_f, image = refs[MATS : MATS + 10]
    wet_out, wet_in, received = refs[MATS + 10 : MATS + 13]
    landing = refs[MATS + 13 : -6]
    send_sem, recv_sem, halo_send, halo_recv, wet_send, wet_recv = refs[-6:]
    rows_s, size = struct.shape
    rows_f = fluid.shape[0]
    bm, bn = size // nr, size // nc
    hb = bm // PARTS
    border = TILE * HALO
    shards = nr * nc
    row, col = lax.axis_index("row"), lax.axis_index("col")
    block = row * nc + col
    following = lax.rem(block + 1, shards)
    previous = lax.rem(block + shards - 1, shards)
    after = (following // nc, lax.rem(following, nc))
    before = (previous // nc, lax.rem(previous, nc))
    row_bits, col_bits = bits_of(nr), bits_of(nc)
    stages = row_bits + col_bits
    my_row = [lax.rem(row // (1 << b), 2) for b in range(row_bits)]
    my_col = [lax.rem(col // (1 << b), 2) for b in range(col_bits)]
    row_peer = [(row + (1 - 2 * my_row[b]) * (1 << b), col) for b in range(row_bits)]
    col_peer = [(row, col + (1 - 2 * my_col[b]) * (1 << b)) for b in range(col_bits)]

    barrier = pltpu.get_barrier_semaphore()

    def device_at(distance):
        other = lax.rem(block + distance, shards)
        return other, (other // nc, lax.rem(other, nc))

    def greet(distance, carry):
        pl.semaphore_signal(barrier, inc=1, device_id=device_at(distance)[1], device_id_type=MESH)
        return carry

    lax.fori_loop(1, shards, greet, 0)
    high_fluid, low_fluid = halves(fluid[...])
    chooser = selector[...].astype(jnp.bfloat16)
    outgoing = jnp.dot(chooser, high_fluid, preferred_element_type=jnp.float32)
    outgoing += jnp.dot(chooser, low_fluid, preferred_element_type=jnp.float32)
    for shard in range(shards):
        wet_out[shard] = outgoing[shard * CAP : (shard + 1) * CAP]
    pl.semaphore_wait(barrier, shards - 1)

    def halo_copy(number, source, target, device):
        return pltpu.make_async_remote_copy(
            src_ref=source,
            dst_ref=target,
            send_sem=halo_send.at[number],
            recv_sem=halo_recv.at[number],
            device_id=device,
            device_id_type=MESH,
        )

    halos = [
        halo_copy(0, struct.at[pl.ds(rows_s - border, border)], halo_s.at[0], after),
        halo_copy(1, struct.at[pl.ds(0, border)], halo_s.at[1], before),
        halo_copy(2, fluid.at[pl.ds(rows_f - border, border)], halo_f.at[0], after),
        halo_copy(3, fluid.at[pl.ds(0, border)], halo_f.at[1], before),
    ]

    def send_wet(distance, carry):
        other, device = device_at(distance)
        pltpu.make_async_remote_copy(
            src_ref=wet_out.at[other],
            dst_ref=wet_in.at[block],
            send_sem=wet_send,
            recv_sem=wet_recv,
            device_id=device,
            device_id_type=MESH,
        ).start()
        return carry

    lax.fori_loop(1, shards, send_wet, 0)
    for copy in halos:
        copy.start()
    wet_in[block] = wet_out[block]
    wet_all = pltpu.make_async_remote_copy(
        src_ref=wet_out.at[pl.ds(0, shards - 1)],
        dst_ref=wet_in.at[pl.ds(0, shards - 1)],
        send_sem=wet_send,
        recv_sem=wet_recv,
        device_id=after,
        device_id_type=MESH,
    )

    def row_order(half):
        order = list(range(row_bits))
        return order if half % 2 == 0 else order[:1] + order[1:][::-1]

    def exchange(half, mat, stage):
        if stage < row_bits:
            order, mine, peers, at = row_order(half), my_row, row_peer, stage
        else:
            order, mine, peers, at = list(range(col_bits)), my_col, col_peer, stage - row_bits
        fixed = sum((mine[b] * (1 << b) for b in order[:at]), 0)
        bit = order[at]
        rest = subset_offsets(order[at + 1 :])
        sent = [fixed + (1 - mine[bit]) * (1 << bit) + extra for extra in rest]
        kept = [fixed + mine[bit] * (1 << bit) + extra for extra in rest]
        return sent, kept, peers[bit]

    def whole_stage(half, mat, stage):
        peer = exchange(half, mat, stage)[2]
        return pltpu.make_async_remote_copy(
            src_ref=landing[stage].at[half, mat],
            dst_ref=landing[stage].at[half, mat],
            send_sem=send_sem.at[half, mat, stage],
            recv_sem=recv_sem.at[half, mat, stage],
            device_id=peer,
            device_id_type=MESH,
        )

    def send(half, mat, stage):
        sent, kept, peer = exchange(half, mat, stage)
        for place, index in enumerate(sent):
            if stage < row_bits:
                source = acc.at[half, mat, index]
            else:
                source = acc.at[half, mat, row, index]
            pltpu.make_async_remote_copy(
                src_ref=source,
                dst_ref=landing[stage].at[half, mat, place],
                send_sem=send_sem.at[half, mat, stage],
                recv_sem=recv_sem.at[half, mat, stage],
                device_id=peer,
                device_id_type=MESH,
            ).start()

    def absorb(half, mat, stage):
        sent, kept, peer = exchange(half, mat, stage)
        whole_stage(half, mat, stage).wait_recv()
        for place, index in enumerate(kept):
            if stage < row_bits:

                def add(c, carry, place=place, index=index):
                    acc[half, mat, index, c] = acc[half, mat, index, c] + landing[stage][half, mat, place, c]
                    return carry

                lax.fori_loop(0, nc, add, 0)
            elif stage < stages - 1:
                acc[half, mat, row, index] = acc[half, mat, row, index] + landing[stage][half, mat, place]
            else:
                outs[mat][pl.ds(half * hb, hb), :] = acc[half, mat, row, index] + landing[stage][half, mat, place]
        if stage < stages - 1:
            send(half, mat, stage + 1)

    def transpose_into(left, source, count):
        def step(k, carry):
            at = pl.ds(pl.multiple_of(k * TILE, TILE), TILE)
            high, low = halves(source[:, at].T)
            left[at, pl.ds(0, count)] = high
            left[at, pl.ds(count, count)] = high
            left[at, pl.ds(2 * count, count)] = low
            return carry

        lax.fori_loop(0, size // TILE, step, 0)

    def columns(c):
        return pl.ds(pl.multiple_of(c * bn, bn), bn)

    def store_image(value, at, count):
        high, low = halves(value)
        image[pl.ds(0, count), at] = high
        image[pl.ds(count, count), at] = low
        image[pl.ds(2 * count, count), at] = high

    def project(left, count, mat):
        def step(c, carry):
            part = jnp.dot(
                left[...], image[pl.ds(0, 3 * count), columns(c)], preferred_element_type=jnp.float32
            )
            for r in range(nr):
                for half in range(PARTS):
                    start = r * bm + half * hb
                    acc[half, mat, r, c] = part[start : start + hb]
            return carry

        lax.fori_loop(0, nc, step, 0)
        for half in range(PARTS):
            send(half, mat, 0)

    def coupled():
        ch, cl = halves(coupling[...])
        wet_all.wait_recv()
        for shard in range(shards):
            received[pl.ds(shard * CAP, CAP), :] = wet_in[shard]

        def step(c, carry):
            at = columns(c)
            rh, rl = halves(received[:, at])
            value = jnp.dot(ch, rh, preferred_element_type=jnp.float32)
            value += jnp.dot(ch, rl, preferred_element_type=jnp.float32)
            value += jnp.dot(cl, rh, preferred_element_type=jnp.float32)
            store_image(value, at, rows_s)
            return carry

        lax.fori_loop(0, nc, step, 0)
        project(left_s, rows_s, 0)

    def place_rows(ext, total, start, value):
        count = value.shape[0]
        high, low = halves(value)
        ext[pl.ds(start, count), :] = high
        ext[pl.ds(total + start, count), :] = low
        ext[pl.ds(2 * total + start, count), :] = high

    def fill_ext(ext, own, halo, first, second):
        total = own.shape[0] + 2 * border
        place_rows(ext, total, border, own[...])
        halos[first].wait_recv()
        halos[second].wait_recv()
        place_rows(ext, total, 0, jnp.where(block > 0, halo[0], 0.0))
        place_rows(ext, total, total - border, jnp.where(block < shards - 1, halo[1], 0.0))

    def sparse_image(tiles, cols, dense, ext, rows, left, mat):
        total = rows + 2 * border
        for i in range(rows // TILE):
            for c in range(total // TILE):
                tile = jnp.zeros((TILE, TILE), jnp.float32)
                for k in range(tiles.shape[1]):
                    tile += jnp.where(cols[i, k] == c, tiles[i, k], 0.0)
                high, low = halves(tile)
                at = pl.ds(i * TILE, TILE)
                dense[at, pl.ds(c * TILE, TILE)] = high
                dense[at, pl.ds(total + c * TILE, TILE)] = high
                dense[at, pl.ds(2 * total + c * TILE, TILE)] = low

        def step(c, carry):
            at = columns(c)
            store_image(jnp.dot(dense[...], ext[:, at], preferred_element_type=jnp.float32), at, rows)
            return carry

        lax.fori_loop(0, nc, step, 0)
        project(left, rows, mat)

    def compute(mat):
        if mat == 0:
            transpose_into(left_s, struct, rows_s)
            coupled()
        elif mat == 1:
            fill_ext(ext_s, struct, halo_s, 0, 1)
            sparse_image(stiff_tiles, struct_cols, tiles_s, ext_s, rows_s, left_s, 1)
        elif mat == 2:
            sparse_image(mass_tiles, struct_cols, tiles_s, ext_s, rows_s, left_s, 2)
        elif mat == 3:
            transpose_into(left_f, fluid, rows_f)
            fill_ext(ext_f, fluid, halo_f, 2, 3)
            sparse_image(fstiff_tiles, fluid_cols, tiles_f, ext_f, rows_f, left_f, 3)
        else:
            sparse_image(fmass_tiles, fluid_cols, tiles_f, ext_f, rows_f, left_f, 4)

    def reduce_stage(mat, stage):
        for half in range(PARTS):
            absorb(half, mat, stage)

    compute(0)
    reduce_stage(0, 0)
    compute(1)
    compute(2)
    reduce_stage(1, 0)
    reduce_stage(0, 1)
    reduce_stage(2, 0)
    reduce_stage(0, 2)
    reduce_stage(1, 1)
    compute(3)
    compute(4)
    reduce_stage(3, 0)
    reduce_stage(4, 0)
    done = {0: 3, 1: 2, 2: 1, 3: 1, 4: 1}
    while any(done[mat] < stages for mat in done):
        for mat in reversed(range(MATS)):
            if done[mat] < stages and (mat == 0 or done[mat] < done[mat - 1]):
                reduce_stage(mat, done[mat])
                done[mat] += 1

    for copy in halos:
        copy.wait_send()
    wet_all.wait_send()
    for mat in range(MATS):
        for half in range(PARTS):
            for stage in range(stages):
                whole_stage(half, mat, stage).wait_send()


def reduced(nr, nc, struct_cols, fluid_cols, *operands):
    struct, fluid = operands[0], operands[1]
    rows_s, size = struct.shape
    rows_f = fluid.shape[0]
    bm, bn = size // nr, size // nc
    hb = bm // PARTS
    row_bits, col_bits = bits_of(nr), bits_of(nc)
    stages = row_bits + col_bits
    shards = nr * nc
    border = TILE * HALO
    total_s, total_f = rows_s + 2 * border, rows_f + 2 * border
    f32, bf16 = jnp.float32, jnp.bfloat16
    landing = [pltpu.VMEM((PARTS, MATS, nr >> (s + 1), nc, hb, bn), f32) for s in range(row_bits)]
    landing += [pltpu.VMEM((PARTS, MATS, nc >> (s + 1), hb, bn), f32) for s in range(col_bits)]
    smem = pl.BlockSpec(memory_space=pltpu.SMEM)
    vmem = pl.BlockSpec(memory_space=pltpu.VMEM)
    return pl.pallas_call(
        functools.partial(kernel, nr, nc),
        out_shape=[jax.ShapeDtypeStruct((bm, bn), f32)] * MATS,
        in_specs=[smem, smem] + [vmem] * len(operands),
        out_specs=[vmem] * MATS,
        scratch_shapes=[
            pltpu.VMEM((PARTS, MATS, nr, nc, hb, bn), f32),
            pltpu.VMEM((2, border, size), f32),
            pltpu.VMEM((2, border, size), f32),
            pltpu.VMEM((size, 3 * rows_s), bf16),
            pltpu.VMEM((size, 3 * rows_f), bf16),
            pltpu.VMEM((rows_s, 3 * total_s), bf16),
            pltpu.VMEM((rows_f, 3 * total_f), bf16),
            pltpu.VMEM((3 * total_s, size), bf16),
            pltpu.VMEM((3 * total_f, size), bf16),
            pltpu.VMEM((3 * rows_s, size), bf16),
            pltpu.VMEM((shards, CAP, size), f32),
            pltpu.VMEM((shards, CAP, size), f32),
            pltpu.VMEM((shards * CAP, size), f32),
            *landing,
            pltpu.SemaphoreType.DMA((PARTS, MATS, stages)),
            pltpu.SemaphoreType.DMA((PARTS, MATS, stages)),
            pltpu.SemaphoreType.DMA((4,)),
            pltpu.SemaphoreType.DMA((4,)),
            pltpu.SemaphoreType.DMA,
            pltpu.SemaphoreType.DMA,
        ],
        compiler_params=pltpu.CompilerParams(
            collective_id=0, has_side_effects=True, vmem_limit_bytes=VMEM_LIMIT
        ),
        name="reduced",
    )(struct_cols, fluid_cols, *operands)


def on_device(
    nr,
    nc,
    struct_basis,
    fluid_basis,
    stiff_tiles,
    mass_tiles,
    fluid_stiff_tiles,
    fluid_mass_tiles,
    struct_cols,
    fluid_cols,
    wet_rows,
    wet_dest,
    coupling,
):
    shards = nr * nc
    destination = wet_dest[:, 0]
    same = destination[:, None] == destination[None, :]
    entry = jnp.arange(destination.shape[0], dtype=jnp.int32)
    earlier = entry[None, :] < entry[:, None]
    slot_index = jnp.sum((same & earlier).astype(jnp.int32), axis=1)
    target = destination * CAP + slot_index
    fluid_row = jnp.arange(fluid_basis.shape[0], dtype=jnp.int32)
    slots = jnp.arange(shards * CAP, dtype=jnp.int32)
    hit = (slots[:, None, None] == target[None, None, :]) & (fluid_row[None, :, None] == wet_rows[None, None, :])
    selector = jnp.any(hit, axis=2).astype(jnp.float32)
    coupling_red, stiff_red, mass_red, fstiff_red, fmass_red = reduced(
        nr,
        nc,
        struct_cols,
        fluid_cols,
        struct_basis,
        fluid_basis,
        stiff_tiles,
        mass_tiles,
        fluid_stiff_tiles,
        fluid_mass_tiles,
        coupling,
        selector,
    )
    return stiff_red, mass_red, fstiff_red, fmass_red, coupling_red


def solution(mesh):
    tiled = P(("row", "col"), None, None, None)
    lined = P(("row", "col"), None)
    return jax.shard_map(
        functools.partial(on_device, mesh.shape["row"], mesh.shape["col"]),
        mesh=mesh,
        in_specs=(lined, lined, tiled, tiled, tiled, tiled, lined, lined, P(("row", "col")), lined, lined),
        out_specs=(P("row", "col"),) * 5,
        check_vma=False,
    )
```

```python
import functools

import jax
import jax.numpy as jnp
from jax import lax
from jax.experimental import pallas as pl
from jax.experimental.pallas import tpu as pltpu
from jax.sharding import PartitionSpec as P

TILE = 128
HALO = 1
CAP = 2
MATS = 5
PARTS = 4
EARLY = {3: (0,), 4: (0, 1)}
VMEM_LIMIT = 67043328
MESH = pl.DeviceIdType.MESH


def halves(value):
    high = value.astype(jnp.bfloat16)
    low = (value - high.astype(jnp.float32)).astype(jnp.bfloat16)
    return high, low


def bits_of(size):
    return size.bit_length() - 1


def subset_offsets(bits):
    offsets = [0]
    for bit in bits:
        offsets = [base + extra for extra in (0, 1 << bit) for base in offsets]
    return offsets


def kernel(
    nr,
    nc,
    struct_cols,
    fluid_cols,
    struct,
    fluid,
    stiff_tiles,
    mass_tiles,
    fstiff_tiles,
    fmass_tiles,
    coupling,
    selector,
    *refs,
):
    outs = refs[0]
    acc, halo_s, halo_f, left_s, left_f, tiles_s, tiles_f, ext_s, ext_f, image = refs[1:11]
    wet_out, wet_in, received = refs[11:14]
    landing = refs[14:-6]
    send_sem, recv_sem, halo_send, halo_recv, wet_send, wet_recv = refs[-6:]
    rows_s, size = struct.shape
    rows_f = fluid.shape[0]
    bm, bn = size // nr, size // nc
    hb = bm // PARTS
    border = TILE * HALO
    shards = nr * nc
    row, col = lax.axis_index("row"), lax.axis_index("col")
    block = row * nc + col
    following = lax.rem(block + 1, shards)
    previous = lax.rem(block + shards - 1, shards)
    after = (following // nc, lax.rem(following, nc))
    before = (previous // nc, lax.rem(previous, nc))
    row_bits, col_bits = bits_of(nr), bits_of(nc)
    stages = row_bits + col_bits
    my_row = [lax.rem(row // (1 << b), 2) for b in range(row_bits)]
    my_col = [lax.rem(col // (1 << b), 2) for b in range(col_bits)]
    row_peer = [(row + (1 - 2 * my_row[b]) * (1 << b), col) for b in range(row_bits)]
    col_peer = [(row, col + (1 - 2 * my_col[b]) * (1 << b)) for b in range(col_bits)]

    barrier = pltpu.get_barrier_semaphore()

    def device_at(distance):
        other = lax.rem(block + distance, shards)
        return other, (other // nc, lax.rem(other, nc))

    def greet(distance, carry):
        pl.semaphore_signal(barrier, inc=1, device_id=device_at(distance)[1], device_id_type=MESH)
        return carry

    lax.fori_loop(1, shards, greet, 0)
    high_fluid, low_fluid = halves(fluid[...])
    chooser = selector[...].astype(jnp.bfloat16)
    outgoing = jnp.dot(chooser, high_fluid, preferred_element_type=jnp.float32)
    outgoing += jnp.dot(chooser, low_fluid, preferred_element_type=jnp.float32)
    for shard in range(shards):
        wet_out[shard] = outgoing[shard * CAP : (shard + 1) * CAP]
    pl.semaphore_wait(barrier, shards - 1)

    def halo_copy(number, source, target, device):
        return pltpu.make_async_remote_copy(
            src_ref=source,
            dst_ref=target,
            send_sem=halo_send.at[number],
            recv_sem=halo_recv.at[number],
            device_id=device,
            device_id_type=MESH,
        )

    halos = [
        halo_copy(0, struct.at[pl.ds(rows_s - border, border)], halo_s.at[0], after),
        halo_copy(1, struct.at[pl.ds(0, border)], halo_s.at[1], before),
        halo_copy(2, fluid.at[pl.ds(rows_f - border, border)], halo_f.at[0], after),
        halo_copy(3, fluid.at[pl.ds(0, border)], halo_f.at[1], before),
    ]

    def send_wet(distance, carry):
        other, device = device_at(distance)
        pltpu.make_async_remote_copy(
            src_ref=wet_out.at[other],
            dst_ref=wet_in.at[block],
            send_sem=wet_send,
            recv_sem=wet_recv,
            device_id=device,
            device_id_type=MESH,
        ).start()
        return carry

    lax.fori_loop(1, shards, send_wet, 0)
    halos[0].start()
    halos[1].start()
    wet_in[block] = wet_out[block]
    wet_all = pltpu.make_async_remote_copy(
        src_ref=wet_out.at[pl.ds(0, shards - 1)],
        dst_ref=wet_in.at[pl.ds(0, shards - 1)],
        send_sem=wet_send,
        recv_sem=wet_recv,
        device_id=after,
        device_id_type=MESH,
    )

    def order_of(half, mat):
        rows = [("row", b) for b in range(row_bits)]
        cols = [("col", b) for b in range(col_bits)]
        if half % 2:
            rows = rows[:1] + rows[1:][::-1]
        if mat in EARLY and half in EARLY[mat]:
            return rows[:1] + cols[:1] + rows[1:] + cols[1:]
        return rows + cols

    def exchange(half, mat, stage):
        order = order_of(half, mat)
        axis, bit = order[stage]
        mine = {"row": my_row, "col": my_col}
        places = {}
        for name in ("row", "col"):
            fixed = sum((mine[name][b] * (1 << b) for at, b in order[:stage] if at == name), 0)
            rest = subset_offsets(sorted(b for at, b in order[stage + 1 :] if at == name))
            places[name] = [fixed + extra for extra in rest]
        sent, kept = dict(places), dict(places)
        sent[axis] = [index + (1 - mine[axis][bit]) * (1 << bit) for index in places[axis]]
        kept[axis] = [index + mine[axis][bit] * (1 << bit) for index in places[axis]]
        peer = (row_peer if axis == "row" else col_peer)[bit]
        return sent, kept, peer

    def whole_stage(half, mat, stage):
        peer = exchange(half, mat, stage)[2]
        return pltpu.make_async_remote_copy(
            src_ref=landing[stage].at[half, mat],
            dst_ref=landing[stage].at[half, mat],
            send_sem=send_sem.at[half, mat, stage],
            recv_sem=recv_sem.at[half, mat, stage],
            device_id=peer,
            device_id_type=MESH,
        )

    def send(half, mat, stage):
        sent, kept, peer = exchange(half, mat, stage)
        width = len(sent["col"])
        for place, r in enumerate(sent["row"]):
            if width == nc:
                pairs = [(acc.at[half, mat, r], landing[stage].at[half, mat, pl.ds(place * nc, nc)])]
            else:
                pairs = [
                    (acc.at[half, mat, r, c], landing[stage].at[half, mat, place * width + at])
                    for at, c in enumerate(sent["col"])
                ]
            for source, target in pairs:
                pltpu.make_async_remote_copy(
                    src_ref=source,
                    dst_ref=target,
                    send_sem=send_sem.at[half, mat, stage],
                    recv_sem=recv_sem.at[half, mat, stage],
                    device_id=peer,
                    device_id_type=MESH,
                ).start()

    def absorb(half, mat, stage):
        sent, kept, peer = exchange(half, mat, stage)
        whole_stage(half, mat, stage).wait_recv()
        width = len(kept["col"])
        for place, r in enumerate(kept["row"]):
            if width == nc:

                def add(c, carry, place=place, r=r):
                    acc[half, mat, r, c] = acc[half, mat, r, c] + landing[stage][half, mat, place * nc + c]
                    return carry

                lax.fori_loop(0, nc, add, 0)
            else:
                for at, c in enumerate(kept["col"]):
                    total = acc[half, mat, r, c] + landing[stage][half, mat, place * width + at]
                    if stage < stages - 1:
                        acc[half, mat, r, c] = total
                    else:
                        outs[mat, pl.ds(half * hb, hb), :] = total
        if stage < stages - 1:
            send(half, mat, stage + 1)

    def transpose_into(left, source, count):
        def step(k, carry):
            at = pl.ds(pl.multiple_of(k * TILE, TILE), TILE)
            high, low = halves(source[:, at].T)
            left[at, pl.ds(0, count)] = high
            left[at, pl.ds(count, count)] = high
            left[at, pl.ds(2 * count, count)] = low
            return carry

        lax.fori_loop(0, size // TILE, step, 0)

    def columns(c):
        return pl.ds(pl.multiple_of(c * bn, bn), bn)

    def store_image(value, at, count):
        high, low = halves(value)
        image[pl.ds(0, count), at] = high
        image[pl.ds(count, count), at] = low
        image[pl.ds(2 * count, count), at] = high

    def project(left, count, mat):
        def step(c, carry):
            part = jnp.dot(
                left[...], image[pl.ds(0, 3 * count), columns(c)], preferred_element_type=jnp.float32
            )
            for r in range(nr):
                for half in range(PARTS):
                    start = r * bm + half * hb
                    acc[half, mat, r, c] = part[start : start + hb]
            return carry

        lax.fori_loop(0, nc, step, 0)
        for half in range(PARTS):
            send(half, mat, 0)

    def coupled():
        ch, cl = halves(coupling[...])
        wet_all.wait_recv()
        for shard in range(shards):
            received[pl.ds(shard * CAP, CAP), :] = wet_in[shard]

        def step(c, carry):
            at = columns(c)
            rh, rl = halves(received[:, at])
            value = jnp.dot(ch, rh, preferred_element_type=jnp.float32)
            value += jnp.dot(ch, rl, preferred_element_type=jnp.float32)
            value += jnp.dot(cl, rh, preferred_element_type=jnp.float32)
            store_image(value, at, rows_s)
            return carry

        lax.fori_loop(0, nc, step, 0)
        project(left_s, rows_s, 0)

    def place_rows(ext, total, start, value):
        count = value.shape[0]
        high, low = halves(value)
        ext[pl.ds(start, count), :] = high
        ext[pl.ds(total + start, count), :] = low
        ext[pl.ds(2 * total + start, count), :] = high

    def fill_ext(ext, own, halo, first, second):
        total = own.shape[0] + 2 * border
        place_rows(ext, total, border, own[...])
        halos[first].wait_recv()
        halos[second].wait_recv()
        if first == 0:
            halos[2].start()
            halos[3].start()
        place_rows(ext, total, 0, jnp.where(block > 0, halo[0], 0.0))
        place_rows(ext, total, total - border, jnp.where(block < shards - 1, halo[1], 0.0))

    def sparse_image(tiles, cols, dense, ext, rows, left, mat):
        total = rows + 2 * border
        for i in range(rows // TILE):
            for c in range(total // TILE):
                tile = jnp.zeros((TILE, TILE), jnp.float32)
                for k in range(tiles.shape[1]):
                    tile += jnp.where(cols[i, k] == c, tiles[i, k], 0.0)
                high, low = halves(tile)
                at = pl.ds(i * TILE, TILE)
                dense[at, pl.ds(c * TILE, TILE)] = high
                dense[at, pl.ds(total + c * TILE, TILE)] = high
                dense[at, pl.ds(2 * total + c * TILE, TILE)] = low

        def step(c, carry):
            at = columns(c)
            store_image(jnp.dot(dense[...], ext[:, at], preferred_element_type=jnp.float32), at, rows)
            return carry

        lax.fori_loop(0, nc, step, 0)
        project(left, rows, mat)

    def compute(mat):
        if mat == 0:
            transpose_into(left_s, struct, rows_s)
            coupled()
        elif mat == 1:
            fill_ext(ext_s, struct, halo_s, 0, 1)
            sparse_image(stiff_tiles, struct_cols, tiles_s, ext_s, rows_s, left_s, 1)
        elif mat == 2:
            sparse_image(mass_tiles, struct_cols, tiles_s, ext_s, rows_s, left_s, 2)
        elif mat == 3:
            transpose_into(left_f, fluid, rows_f)
            fill_ext(ext_f, fluid, halo_f, 2, 3)
            sparse_image(fstiff_tiles, fluid_cols, tiles_f, ext_f, rows_f, left_f, 3)
        else:
            sparse_image(fmass_tiles, fluid_cols, tiles_f, ext_f, rows_f, left_f, 4)

    def reduce_stage(mat, stage):
        for half in range(PARTS):
            absorb(half, mat, stage)

    compute(0)
    reduce_stage(0, 0)
    compute(1)
    reduce_stage(1, 0)
    compute(2)
    reduce_stage(0, 1)
    reduce_stage(2, 0)
    reduce_stage(0, 2)
    reduce_stage(1, 1)
    compute(3)
    compute(4)
    reduce_stage(3, 0)
    reduce_stage(4, 0)
    done = {0: 3, 1: 2, 2: 1, 3: 1, 4: 1}
    while any(done[mat] < stages for mat in done):
        for mat in reversed(range(MATS)):
            if done[mat] < stages and (mat == 0 or done[mat] < done[mat - 1]):
                reduce_stage(mat, done[mat])
                done[mat] += 1

    for copy in halos:
        copy.wait_send()
    wet_all.wait_send()
    for mat in range(MATS):
        for half in range(PARTS):
            for stage in range(stages):
                whole_stage(half, mat, stage).wait_send()


def reduced(nr, nc, struct_cols, fluid_cols, *operands):
    struct, fluid = operands[0], operands[1]
    rows_s, size = struct.shape
    rows_f = fluid.shape[0]
    bm, bn = size // nr, size // nc
    hb = bm // PARTS
    row_bits, col_bits = bits_of(nr), bits_of(nc)
    stages = row_bits + col_bits
    shards = nr * nc
    border = TILE * HALO
    total_s, total_f = rows_s + 2 * border, rows_f + 2 * border
    f32, bf16 = jnp.float32, jnp.bfloat16
    landing = [pltpu.VMEM((PARTS, MATS, shards >> (s + 1), hb, bn), f32) for s in range(stages)]
    smem = pl.BlockSpec(memory_space=pltpu.SMEM)
    vmem = pl.BlockSpec(memory_space=pltpu.VMEM)
    return pl.pallas_call(
        functools.partial(kernel, nr, nc),
        out_shape=jax.ShapeDtypeStruct((MATS, bm, bn), f32),
        in_specs=[smem, smem] + [vmem] * len(operands),
        out_specs=vmem,
        scratch_shapes=[
            pltpu.VMEM((PARTS, MATS, nr, nc, hb, bn), f32),
            pltpu.VMEM((2, border, size), f32),
            pltpu.VMEM((2, border, size), f32),
            pltpu.VMEM((size, 3 * rows_s), bf16),
            pltpu.VMEM((size, 3 * rows_f), bf16),
            pltpu.VMEM((rows_s, 3 * total_s), bf16),
            pltpu.VMEM((rows_f, 3 * total_f), bf16),
            pltpu.VMEM((3 * total_s, size), bf16),
            pltpu.VMEM((3 * total_f, size), bf16),
            pltpu.VMEM((3 * rows_s, size), bf16),
            pltpu.VMEM((shards, CAP, size), f32),
            pltpu.VMEM((shards, CAP, size), f32),
            pltpu.VMEM((shards * CAP, size), f32),
            *landing,
            pltpu.SemaphoreType.DMA((PARTS, MATS, stages)),
            pltpu.SemaphoreType.DMA((PARTS, MATS, stages)),
            pltpu.SemaphoreType.DMA((4,)),
            pltpu.SemaphoreType.DMA((4,)),
            pltpu.SemaphoreType.DMA,
            pltpu.SemaphoreType.DMA,
        ],
        compiler_params=pltpu.CompilerParams(
            collective_id=0, has_side_effects=True, vmem_limit_bytes=VMEM_LIMIT
        ),
        name="reduced",
    )(struct_cols, fluid_cols, *operands)


def on_device(
    nr,
    nc,
    struct_basis,
    fluid_basis,
    stiff_tiles,
    mass_tiles,
    fluid_stiff_tiles,
    fluid_mass_tiles,
    struct_cols,
    fluid_cols,
    wet_rows,
    wet_dest,
    coupling,
):
    shards = nr * nc
    destination = wet_dest[:, 0]
    same = destination[:, None] == destination[None, :]
    entry = jnp.arange(destination.shape[0], dtype=jnp.int32)
    earlier = entry[None, :] < entry[:, None]
    slot_index = jnp.sum((same & earlier).astype(jnp.int32), axis=1)
    target = destination * CAP + slot_index
    fluid_row = jnp.arange(fluid_basis.shape[0], dtype=jnp.int32)
    slots = jnp.arange(shards * CAP, dtype=jnp.int32)
    hit = (slots[:, None, None] == target[None, None, :]) & (fluid_row[None, :, None] == wet_rows[None, None, :])
    selector = jnp.any(hit, axis=2).astype(jnp.float32)
    coupling_red, stiff_red, mass_red, fstiff_red, fmass_red = reduced(
        nr,
        nc,
        struct_cols,
        fluid_cols,
        struct_basis,
        fluid_basis,
        stiff_tiles,
        mass_tiles,
        fluid_stiff_tiles,
        fluid_mass_tiles,
        coupling,
        selector,
    )
    return stiff_red, mass_red, fstiff_red, fmass_red, coupling_red


def solution(mesh):
    tiled = P(("row", "col"), None, None, None)
    lined = P(("row", "col"), None)
    return jax.shard_map(
        functools.partial(on_device, mesh.shape["row"], mesh.shape["col"]),
        mesh=mesh,
        in_specs=(lined, lined, tiled, tiled, tiled, tiled, lined, lined, P(("row", "col")), lined, lined),
        out_specs=(P("row", "col"),) * 5,
        check_vma=False,
    )
```
